128 devices in a mesh: ctx: 32 (over x_hi, z, y), tp: 4 (over x_lo, core).
Axes of the slice: x: 4 (x_hi: 2, x_lo: 2; x = x_hi * 2 + x_lo), y: 4, z: 4, core: 2. Of those that a mesh axis runs over, the one named last changes fastest.
Arguments:
- qkv: bfloat16 [3, 8192, 4096], P(None, 'ctx', 'tp'), may hold values from -6 to 6
- filters: bfloat16 [256, 128], P('tp'), may hold values from -0.5 to 0.5
- w_out: bfloat16 [4096, 4096], P(None, 'tp'), may hold values from -0.09375 to 0.09375
- cotangent: bfloat16 [8192, 4096], P(('ctx', 'tp')), may hold values from -24 to 24
- doc_lens: int32 [64], replicated, may hold values from 1 to 384, 8192 in all
Outputs:
- grad_qkv: bfloat16 [3, 8192, 4096], P(None, 'ctx', 'tp')
- grad_filters: float32 [256, 128], P('tp')
- grad_w_out: float32 [4096, 4096], P('ctx', 'tp')
The draws below stay inside these ranges and needn't reach their ends.
All inputs are finite; a program needn't handle non-finite values.
Results may differ from the reference program's by a relative error of at most 0.005.
Values may be sent and summed in bfloat16 or wider, within the bound.
A program may use at most 128 MiB of HBM per device.

```python
import math
import jax
import jax.numpy as jnp
import numpy as np
from jax import lax

D = 4096
GROUP = 16
TAPS = 128
SPAN = 128
GROUPS = 256
TOKENS = 8192
NDOCS = 64
MOST = 384
N_CTX = 32


def raised(result, key, source, target, blocks, factor):
    owner, partner = [(jnp.arange(result.shape[axis_at]) // (result.shape[axis_at] // blocks)).reshape([-1 if axis == axis_at else 1 for axis in range(result.ndim)]) for axis_at in (source, target)]
    chosen = jax.random.permutation(key, blocks)[partner]
    strong = (owner == chosen) | (owner == (partner + blocks // 2) % blocks)
    return jnp.where(strong, factor * result, result)


def steps_of(stream_key, shape, split, low, largest):
    loudness, own = 1.0, jax.random.fold_in(stream_key, 6)
    for position, blocks in split:
        steps = jnp.exp(jax.random.uniform(jax.random.fold_in(own, position), (blocks,), jnp.float32, low / len(split), largest / len(split)))
        loudness = loudness * jnp.repeat(steps, shape[position] // blocks).reshape([-1 if axis == position else 1 for axis in range(len(shape))])
    return loudness


def profile(amount, total, bound, skew):
    loads = [(1 << 20) // math.isqrt(standing ** skew) + 1 for standing in range(2, amount + 1)]
    spare, given = total - bound - (amount - 1), [1] * (amount - 1)
    while spare > 0:
        free = [i for i in range(amount - 1) if given[i] < bound]
        whole, budget = sum([loads[i] for i in free]), spare
        for i in free:
            more = min(bound - given[i], max(1, budget * loads[i] // whole), spare)
            given[i] = given[i] + more
            spare = spare - more
    return np.array([bound] + given)


def uneven(stream_key, count, total, bound, skew):
    if count == 2:
        one = jax.random.randint(stream_key, (), max(1, total - bound), min(bound, total - 1) + 1)
        return jnp.stack([one, total - one])
    lengths = jnp.asarray(profile(count, total, bound, skew), jnp.int32)
    twos = (count - 1) // 2
    donor, sink = lengths[1:1 + 2 * twos:2], lengths[2:2 + 2 * twos:2]
    room = jnp.minimum(donor - 1, bound - sink)
    shifted = jax.random.randint(jax.random.fold_in(stream_key, 1), (twos,), 0, 1 << 20) % (room + 1)
    lengths = lengths.at[1:1 + 2 * twos:2].set(donor - shifted).at[2:2 + 2 * twos:2].set(sink + shifted)
    return lengths[jax.random.permutation(jax.random.fold_in(stream_key, 2), count)]


def centred(rng, extent, scale, reach, split=(), kind=jnp.bfloat16):
    entries = jax.random.normal(rng, extent, jnp.float32) * scale
    if len(split) > 0:
        entries = steps_of(rng, extent, split, -0.22, 0.18) * entries
    return jnp.clip(entries, min=-reach, max=reach).astype(kind)


def gaussian_with(own_key, extent, scale, reach, split, heavy, kind=jnp.bfloat16):
    result = scale * jax.random.normal(own_key, extent, jnp.float32)
    if split:
        result = result * steps_of(own_key, extent, split, -0.22, 0.18)
    return jnp.clip(raised(result, jax.random.fold_in(own_key, 3), *heavy), -reach, reach).astype(kind)


def setup_inputs(seed: int = 0) -> dict:
    streams_of = jax.random.split(jax.random.key(seed), 6)
    return {
        "qkv": centred(streams_of[0], (3, TOKENS, D), 1.0, 6.0, ((1, 32), (2, 4))),
        "filters": centred(streams_of[1], (GROUPS, TAPS), TAPS ** -0.5, 0.5, ((0, 4),)),
        "w_out": centred(streams_of[2], (D, D), D ** -0.5, 0.09375, ((1, 4),)),
        "cotangent": gaussian_with(streams_of[3], (TOKENS, D), 1.0, 24.0, ((0, 128),), (0, 1, 128, 5.5)),
        "doc_lens": uneven(streams_of[4], NDOCS, TOKENS, MOST, 1).astype(jnp.int32),
    }


def banded(filters):
    groups, tap_count = filters.shape
    width = 2 * tap_count
    blank = jnp.zeros((groups, 1), filters.dtype)
    tailing = jnp.zeros((groups, width - tap_count), filters.dtype)
    pattern = jnp.concatenate([blank, jnp.flip(filters, axis=1), tailing], axis=1)
    tiled = jnp.broadcast_to(pattern[:, None, :], (groups, tap_count, width + 1)).reshape(groups, tap_count * (width + 1))
    return tiled[:, :tap_count * width].reshape(groups, tap_count, width)

def diagonals(products):
    groups, tap_count, width = products.shape
    flattened = jnp.pad(products.reshape(groups, tap_count * width), ((0, 0), (0, tap_count)))
    sheared = flattened.reshape(groups, tap_count, width + 1)[:, :, 1:tap_count + 1]
    return jnp.flip(lax.optimization_barrier(jnp.sum(sheared, axis=1)), axis=1)

def doc_reach(positions, doc_lens):
    starts = (jnp.cumsum(doc_lens) - doc_lens).astype(jnp.int32)
    below = jnp.where(starts[None, :] <= positions[:, None], starts[None, :], 0)
    return (positions - lax.optimization_barrier(jnp.max(below, axis=1))).astype(jnp.int32)

def band_mask(doc_offset, tap_count, dtype):
    row_ids = lax.broadcasted_iota(jnp.int32, (tap_count, 2 * tap_count), 0)
    col_ids = lax.broadcasted_iota(jnp.int32, (tap_count, 2 * tap_count), 1)
    return (row_ids - col_ids + tap_count <= doc_offset[:, None]).astype(dtype)

def to_natural(array):
    leading = array.shape[:-2]
    chans = array.shape[-1]
    paired = array.reshape(leading + (N_CTX, 2, SPAN, chans))
    first_half = paired[..., 0, :, :]
    second_half = jnp.flip(paired[..., 1, :, :], axis=-3)
    return jnp.concatenate([first_half, second_half], axis=-3).reshape(leading + (TOKENS, chans))

def to_stored(array):
    leading = array.shape[:-2]
    chans = array.shape[-1]
    pieces = array.reshape(leading + (2 * N_CTX, SPAN, chans))
    first_half = pieces[..., :N_CTX, :, :]
    second_half = jnp.flip(pieces[..., N_CTX:, :, :], axis=-3)
    return jnp.stack([first_half, second_half], axis=-3).reshape(leading + (TOKENS, chans))

def reference(qkv, filters, w_out, cotangent, doc_lens):
    natural = to_natural(qkv)
    queries, keys, values = (natural[0], natural[1], natural[2])
    arriving = to_natural(cotangent)
    positions = jnp.arange(TOKENS, dtype=jnp.int32)
    doc_offset = doc_reach(positions, doc_lens)
    hidden = (keys.astype(jnp.float32) * values.astype(jnp.float32)).astype(jnp.bfloat16)
    grad_y = jnp.dot(arriving, w_out, preferred_element_type=jnp.float32)
    grad_c = (queries.astype(jnp.float32) * grad_y).astype(jnp.bfloat16)
    kernel_base = banded(filters.astype(jnp.float32))
    padded_h = jnp.concatenate([jnp.zeros((TAPS, D), jnp.bfloat16), hidden], axis=0)
    exact = lax.Precision.HIGHEST

    def one_block(block_index):
        start = (block_index * TAPS).astype(jnp.int32)
        window = lax.dynamic_slice_in_dim(padded_h, start, 2 * TAPS, 0).astype(jnp.float32).reshape(2 * TAPS, GROUPS, GROUP)
        rows_grad = lax.dynamic_slice_in_dim(grad_c, start, TAPS, 0).astype(jnp.float32).reshape(TAPS, GROUPS, GROUP)
        keep = band_mask(lax.dynamic_slice_in_dim(doc_offset, start, TAPS, 0), TAPS, jnp.float32)
        kernel = kernel_base * keep[None]
        conv_rows = jnp.einsum('gij,jgc->igc', kernel, window, precision=exact).reshape(TAPS, D)
        spread = jnp.einsum('gij,igc->jgc', kernel, rows_grad, precision=exact).reshape(2 * TAPS, D)
        products = jnp.einsum('igc,jgc->gij', rows_grad, window, precision=exact)
        return (conv_rows, spread[:TAPS], spread[TAPS:], diagonals(products * keep[None]))
    conv_blocks, spill_rows, own_rows, filter_parts = lax.map(one_block, jnp.arange(TOKENS // TAPS, dtype=jnp.int32))
    conv_out = conv_blocks.reshape(TOKENS, D)
    following = jnp.concatenate([spill_rows[1:], jnp.zeros((1, TAPS, D), jnp.float32)], axis=0)
    grad_h = (own_rows + following).reshape(TOKENS, D)
    grad_q = (grad_y * conv_out).astype(jnp.bfloat16)
    grad_k = (grad_h * values.astype(jnp.float32)).astype(jnp.bfloat16)
    grad_v = (grad_h * keys.astype(jnp.float32)).astype(jnp.bfloat16)
    grad_qkv = to_stored(jnp.stack([grad_q, grad_k, grad_v]))
    grad_scale = 1.0 / math.sqrt(TOKENS)
    grad_filters = lax.optimization_barrier(jnp.sum(filter_parts, axis=0)) * grad_scale
    gated = (queries.astype(jnp.float32) * conv_out).astype(jnp.bfloat16)
    grad_w = jnp.dot(arriving.T, gated, preferred_element_type=jnp.float32) * grad_scale
    return (grad_qkv, grad_filters, grad_w)
```

```python
import functools
import math

import jax
import jax.numpy as jnp
from jax import lax
from jax.experimental import pallas as pl
from jax.experimental.pallas import tpu as pltpu
from jax.sharding import PartitionSpec as P

LANES = 128
TAPS = 128
GW = 16
PER = LANES // GW


def doc_reach(positions, doc_lens):
    starts = jnp.cumsum(doc_lens) - doc_lens
    below = jnp.where(starts[None, :] <= positions[:, None], starts[None, :], 0)
    return positions - jnp.max(below, axis=1)


def grid_ids():
    rows = lax.broadcasted_iota(jnp.int32, (TAPS, TAPS), 0)
    cols = lax.broadcasted_iota(jnp.int32, (TAPS, TAPS), 1)
    return rows, cols


def sheared(row):
    return pltpu.roll(jnp.broadcast_to(row, (TAPS, TAPS)), 0, 1, stride=1, stride_axis=0)


def window_masks(reach, turned=False):
    rows, cols = grid_ids()
    if turned:
        rows = TAPS - 1 - rows
    prev = (rows < cols) & (rows - cols + TAPS <= reach)
    own = (rows >= cols) & (rows - cols <= reach)
    return prev, own


def conv_tile(h_ref, halo_ref, frev_ref, ocol_ref, q_ref, c_ref, y_ref, stack_ref):
    group = lax.broadcasted_iota(jnp.int32, (TAPS, LANES), 1) // GW
    masks = [window_masks(ocol_ref[a * TAPS : (a + 1) * TAPS, :]) for a in range(2)]
    for g in range(PER):
        circ = sheared(frev_ref[g : g + 1, :])
        for a in range(2):
            prev, own = masks[a]
            rows = slice(g * TAPS, (g + 1) * TAPS)
            stack_ref[a, rows, :TAPS] = jnp.where(prev, circ, 0.0).astype(jnp.bfloat16)
            stack_ref[a, rows, TAPS:] = jnp.where(own, circ, 0.0).astype(jnp.bfloat16)
    for a in range(2):
        span = slice(a * TAPS, (a + 1) * TAPS)
        window = jnp.concatenate([halo_ref[span, :], h_ref[span, :]], axis=0)
        out = jnp.dot(stack_ref[a], window, preferred_element_type=jnp.float32)
        c = out[:TAPS]
        for g in range(1, PER):
            c = jnp.where(group == g, out[g * TAPS : (g + 1) * TAPS], c)
        c_ref[span, :] = c
        y_ref[span, :] = (q_ref[0, span, :].astype(jnp.float32) * c).astype(jnp.bfloat16)


def back_tile(
    kv_ref, h_ref, halo_ref, dc_ref, next_ref, dy_ref, c_ref, f_ref, ocol_ref, orow_ref,
    out_ref, gf_ref, stack_ref, mask_ref,
):
    group = lax.broadcasted_iota(jnp.int32, (TAPS, LANES), 1) // GW
    rows, cols = grid_ids()
    spread = []
    for a in range(2):
        mine = orow_ref[a : a + 1, :]
        following = orow_ref[2 + a : 3 + a, :]
        own = (cols >= rows) & (cols - rows <= mine)
        prev = (cols < rows) & (cols - rows + TAPS <= following)
        spread.append((own, prev))
    for g in range(PER):
        circ = sheared(f_ref[g : g + 1, :])
        for a in range(2):
            own, prev = spread[a]
            part = slice(g * TAPS, (g + 1) * TAPS)
            stack_ref[a, part, :TAPS] = jnp.where(own, circ, 0.0).astype(jnp.bfloat16)
            stack_ref[a, part, TAPS:] = jnp.where(prev, circ, 0.0).astype(jnp.bfloat16)
    turn = jnp.where(rows + cols == TAPS - 1, 1.0, 0.0).astype(jnp.bfloat16)
    for a in range(2):
        span = slice(a * TAPS, (a + 1) * TAPS)
        pair = jnp.concatenate([dc_ref[span, :], next_ref[span, :]], axis=0)
        out = jnp.dot(stack_ref[a], pair, preferred_element_type=jnp.float32)
        dh = out[:TAPS]
        for g in range(1, PER):
            dh = jnp.where(group == g, out[g * TAPS : (g + 1) * TAPS], dh)
        out_ref[0, span, :] = (dy_ref[span, :] * c_ref[span, :]).astype(jnp.bfloat16)
        out_ref[1, span, :] = (dh * kv_ref[1, span, :].astype(jnp.float32)).astype(jnp.bfloat16)
        out_ref[2, span, :] = (dh * kv_ref[0, span, :].astype(jnp.float32)).astype(jnp.bfloat16)
        dc = jnp.dot(turn, dc_ref[span, :], preferred_element_type=jnp.float32)
        for g in range(PER):
            mask_ref[a, g * TAPS : (g + 1) * TAPS, :] = jnp.where(group == g, dc, 0.0).astype(
                jnp.bfloat16
            )
    products = []
    for a in range(2):
        span = slice(a * TAPS, (a + 1) * TAPS)
        window = jnp.concatenate([halo_ref[span, :], h_ref[span, :]], axis=0)
        products.append(
            lax.dot_general(
                mask_ref[a], window, (((1,), (1,)), ((), ())), preferred_element_type=jnp.float32
            )
        )
    masks = [window_masks(ocol_ref[(2 + a) * TAPS : (3 + a) * TAPS, :], True) for a in range(2)]
    for g in range(PER):
        part = slice(g * TAPS, (g + 1) * TAPS)
        total = jnp.zeros((TAPS, TAPS), jnp.float32)
        for a in range(2):
            prev, own = masks[a]
            total = total + jnp.where(prev, products[a][part, :TAPS], 0.0)
            total = total + jnp.where(own, products[a][part, TAPS:], 0.0)
        lined = pltpu.roll(total, 1, 1, stride=1, stride_axis=0)
        gf_ref[g : g + 1, :] = jnp.sum(lined, axis=0, keepdims=True)


def lane_tile(rows):
    return pl.BlockSpec((rows, LANES), lambda i: (0, i))


def whole(shape):
    return pl.BlockSpec(shape, lambda i: tuple(0 for _ in shape))


def convolve(h, halo, frev, ocol, qkv):
    rows, width = h.shape
    return pl.pallas_call(
        conv_tile,
        grid=(width // LANES,),
        in_specs=[
            lane_tile(rows), lane_tile(rows),
            pl.BlockSpec((PER, TAPS), lambda i: (i, 0)),
            whole(ocol.shape),
            pl.BlockSpec((1, rows, LANES), lambda i: (0, 0, i)),
        ],
        out_specs=[lane_tile(rows), lane_tile(rows)],
        out_shape=[
            jax.ShapeDtypeStruct((rows, width), jnp.float32),
            jax.ShapeDtypeStruct((rows, width), jnp.bfloat16),
        ],
        scratch_shapes=[pltpu.VMEM((2, PER * TAPS, 2 * TAPS), jnp.bfloat16)],
        cost_estimate=pl.CostEstimate(
            flops=2 * 2 * PER * TAPS * 2 * TAPS * LANES * 8, bytes_accessed=4 << 20, transcendentals=0
        ),
    )(h, halo, frev, ocol, qkv)


def pull_back(qkv, h, halo, dc, following, dy, c, filt, ocol, orow):
    rows, width = h.shape
    return pl.pallas_call(
        back_tile_from,
        grid=(width // LANES,),
        in_specs=[
            pl.BlockSpec((1, rows, LANES), lambda i: (1, 0, i)),
            pl.BlockSpec((1, rows, LANES), lambda i: (2, 0, i)),
            lane_tile(rows), lane_tile(rows), lane_tile(rows), lane_tile(rows),
            lane_tile(rows), lane_tile(rows),
            pl.BlockSpec((PER, TAPS), lambda i: (i, 0)),
            whole(ocol.shape), whole(orow.shape),
        ],
        out_specs=[
            pl.BlockSpec((3, rows, LANES), lambda i: (0, 0, i)),
            pl.BlockSpec((PER, TAPS), lambda i: (i, 0)),
        ],
        out_shape=[
            jax.ShapeDtypeStruct((3, rows, width), jnp.bfloat16),
            jax.ShapeDtypeStruct((width // GW, TAPS), jnp.float32),
        ],
        scratch_shapes=[
            pltpu.VMEM((2, PER * TAPS, 2 * TAPS), jnp.bfloat16),
            pltpu.VMEM((2, PER * TAPS, LANES), jnp.bfloat16),
        ],
        cost_estimate=pl.CostEstimate(
            flops=4 * 2 * PER * TAPS * 2 * TAPS * LANES * 8, bytes_accessed=8 << 20, transcendentals=0
        ),
    )(qkv, qkv, h, halo, dc, following, dy, c, filt, ocol, orow)


class Pair:
    def __init__(self, first, second):
        self.parts = (first, second)

    def __getitem__(self, key):
        return self.parts[key[0]][(0,) + key[1:]]


def back_tile_from(k_ref, v_ref, *refs):
    back_tile(Pair(k_ref, v_ref), *refs)


def shift(cells, up):
    count = lax.axis_size("ctx")
    pairs = [(i, i + 1) if up else (i + 1, i) for i in range(count - 1)]
    return lax.ppermute(cells, "ctx", pairs)


def local(qkv, filters, w_out, cotangent, doc_lens):
    tok_ctx, width = qkv.shape[1:]
    n_ctx = lax.axis_size("ctx")
    rank = lax.axis_index("ctx")
    last = rank == n_ctx - 1
    tokens = tok_ctx * n_ctx
    full_cot = lax.all_gather(cotangent, "tp", axis=0, tiled=True)
    queries = qkv[0]
    hidden = (qkv[1].astype(jnp.float32) * qkv[2].astype(jnp.float32)).astype(jnp.bfloat16)
    tail_first = shift(hidden[:TAPS], True)
    tail_second = jnp.where(last, hidden[:TAPS], shift(hidden[TAPS:], False))
    halo = jnp.concatenate([tail_first, tail_second], axis=0)
    ids = jnp.arange(TAPS, dtype=jnp.int32)
    starts = jnp.stack([rank, 2 * n_ctx - 1 - rank, rank + 1, 2 * n_ctx - rank]) * TAPS
    reach = doc_reach((starts[:, None] + ids[None, :]).reshape(4 * TAPS), doc_lens)
    orow = reach.reshape(4, TAPS)
    ocol = jnp.concatenate([orow[:2], jnp.flip(orow[:2], axis=1)], axis=0).reshape(4 * TAPS, 1)
    filt = filters.astype(jnp.float32)
    frev = jnp.concatenate([filt[:, :1], jnp.flip(filt[:, 1:], axis=1)], axis=1)
    c, y = convolve(hidden, halo, frev, ocol, qkv)
    scale = 1.0 / math.sqrt(tokens)
    partial = lax.dot_general(
        full_cot, y, (((0,), (0,)), ((), ())), preferred_element_type=jnp.float32
    )
    grad_w = lax.psum_scatter(partial, "ctx", scatter_dimension=0, tiled=True) * scale
    grad_y = jnp.dot(full_cot, w_out, preferred_element_type=jnp.float32)
    grad_c = (queries.astype(jnp.float32) * grad_y).astype(jnp.bfloat16)
    head_first = jnp.where(last, grad_c[TAPS:], shift(grad_c[:TAPS], False))
    head_second = shift(grad_c[TAPS:], True)
    following = jnp.concatenate([head_first, head_second], axis=0)
    grad_qkv, gf = pull_back(qkv, hidden, halo, grad_c, following, grad_y, c, filt, ocol, orow)
    gf = lax.psum(gf, "ctx")
    gf = jnp.concatenate([gf[:, :1], jnp.flip(gf[:, 1:], axis=1)], axis=1) * scale
    return (grad_qkv, gf, grad_w)


def solution(mesh):
    return jax.shard_map(
        local,
        mesh=mesh,
        in_specs=(P(None, "ctx", "tp"), P("tp", None), P(None, "tp"), P(("ctx", "tp"), None), P()),
        out_specs=(P(None, "ctx", "tp"), P("tp", None), P("ctx", "tp")),
        check_vma=False,
    )
```
